256 devices in a mesh: inp: 4 (over y_hi, core), dep: 8 (over x, y_lo), out: 8 (over z).
Axes of the slice: x: 4, y: 4 (y_hi: 2, y_lo: 2; y = y_hi * 2 + y_lo), z: 8, core: 2. Of those that a mesh axis runs over, the one named last changes fastest.
Arguments:
- tokens: bfloat16 [1024, 16384], P('inp', 'out'), may hold values from -6 to 6
- gate_up_weight: bfloat16 [16384, 2, 28672], P('out', None, ('inp', 'dep')), may hold values from -0.046875 to 0.046875
- down_weight: bfloat16 [28672, 16384], P(('inp', 'dep'), 'out'), may hold values from -0.03125 to 0.03125
Outputs:
- layer_output: bfloat16 [1024, 16384], P(('inp', 'dep'), 'out')
The draws below stay inside these ranges and needn't reach their ends.
All inputs are finite; a program needn't handle non-finite values.
Results may differ from the reference program's by a relative error of at most 0.0049.
Values may be sent and summed in bfloat16 or wider, within the bound.
A program may use at most 128 MiB of HBM per device.

```python
import jax
import jax.numpy as jnp

D = 16384
FF = 28672
TOKENS = 1024


def level_of(own_key, shape, split, smallest, high):
    loudness, own = 1.0, jax.random.fold_in(own_key, 6)
    for dim, shards_of in split:
        heights = jnp.exp(jax.random.uniform(jax.random.fold_in(own, dim), (shards_of,), jnp.float32, smallest / len(split), high / len(split)))
        loudness = loudness * jnp.repeat(heights, shape[dim] // shards_of).reshape([-1 if axis == dim else 1 for axis in range(len(shape))])
    return loudness


def gaussian(key, dims, width, most, split=(), dtype=jnp.bfloat16):
    values = width * jax.random.normal(key, dims, jnp.float32)
    if split:
        values = values * level_of(key, dims, split, -0.22, 0.18)
    return jnp.clip(values, -most, most).astype(dtype)


def setup_inputs(seed: int = 0) -> dict:
    streams_of = jax.random.split(jax.random.key(seed), 4)
    tokens = gaussian(streams_of[0], (TOKENS, D), 1.0, 6.0, ((0, 4), (1, 8)))
    gate_up_weight = gaussian(streams_of[1], (D, 2, FF), D ** -0.5, 0.046875, ((0, 8), (2, 32)))
    down_weight = gaussian(streams_of[2], (FF, D), FF ** -0.5, 0.03125, ((0, 32), (1, 8)))
    return dict(tokens=tokens, gate_up_weight=gate_up_weight, down_weight=down_weight)


def reference(tokens, gate_up_weight, down_weight):
    flat_weight = gate_up_weight.reshape(D, 2 * FF)
    projected = jnp.dot(tokens, flat_weight, preferred_element_type=jnp.float32)
    projected = projected.reshape(tokens.shape[0], 2, FF)
    hidden = (jax.nn.silu(projected[:, 0, :]) * projected[:, 1, :]).astype(jnp.bfloat16)
    result = jnp.dot(hidden, down_weight, preferred_element_type=jnp.float32)
    return result.astype(jnp.bfloat16)
```

```python
import jax
import jax.numpy as jnp
from jax import lax
from jax.experimental import pallas as pl
from jax.experimental.pallas import tpu as pltpu
from jax.sharding import PartitionSpec as P

MESH = pl.DeviceIdType.MESH
BF16, F32 = jnp.bfloat16, jnp.float32
UNITS, NZ, NX, ROWS = 4, 8, 4, 32
LANES = 128
START = (0, 4, 7, 10)


def encode(v):
    return (v * jnp.abs(v)).astype(BF16)


def decode(v):
    v = v.astype(F32)
    root = jnp.sqrt(jnp.abs(v))
    return jnp.where(v < 0, -root, root)


def kernel(
    tok, gate_up, down, out,
    X, raw, flat, W, D, PS, SA, SB, RA, RB, HA, HB, own, pair_out, pair_in, xs, xr, ys, yr,
    ld_sem, w_sem, tk_s, tk_r, rs_s, rs_r, ag_s, ag_r, pr_s, pr_r, x_s, x_r, y_s, y_r,
):
    inp, dep, z = lax.axis_index("inp"), lax.axis_index("dep"), lax.axis_index("out")
    x, l = dep // 2, lax.rem(dep, 2)
    h, c = inp // 2, lax.rem(inp, 2)
    dep_l = x * 2 + (1 - l)
    partner = (h * 2 + (1 - c), dep, z)
    y_near = (inp, dep_l, z)
    y_far = ((1 - h) * 2 + c, dep, z)
    cross = ((1 - h) * 2 + c, dep_l, z)
    x_next = (inp, lax.rem(dep + 2, 8), z)
    x_prev = (inp, lax.rem(dep + 6, 8), z)
    z_next = (inp, dep, lax.rem(z + 1, NZ))
    z_prev = (inp, dep, lax.rem(z + NZ - 1, NZ))
    unit_half = ((0, 1 - l), (1, l), (1, 1 - l), (0, l))
    unit_target = (y_near, y_far, cross)

    blocks_a = SA.shape[-1] // (2 * LANES)
    blocks = raw.shape[0]
    wide = (SA.shape[-1], SB.shape[-1])
    first = (0, SA.shape[-1])
    sends = (SA, SB)
    receives = (RA, RB)
    hidden = (HA, HB)
    started = []

    def weight_copy(j):
        columns = pl.ds(pl.multiple_of(j * LANES, LANES), LANES)
        return pltpu.make_async_copy(gate_up.at[:, :, columns], raw.at[j], w_sem.at[j])

    def own_copy(q):
        lp = (1 - l) if q == 0 else l
        return pltpu.make_async_copy(tok.at[:, lp], X.at[0, :, lp], ld_sem.at[q])

    down_copy = pltpu.make_async_copy(down, D, ld_sem.at[2])

    def remote(src, dst, s, r, device):
        return pltpu.make_async_remote_copy(
            src_ref=src, dst_ref=dst, send_sem=s, recv_sem=r, device_id=device, device_id_type=MESH
        )

    def go(copy):
        copy.start()
        started.append(copy)

    own_copy(0).start()
    for j in range(blocks):
        weight_copy(j).start()
    own_copy(1).start()
    down_copy.start()

    barrier = pltpu.get_barrier_semaphore()
    peers = (partner, y_near, y_far, cross, x_next, x_prev, z_next, z_prev)
    for peer in peers:
        pl.semaphore_signal(barrier, inc=1, device_id=peer, device_id_type=MESH)
    pl.semaphore_wait(barrier, len(peers))

    def tok_pair(q):
        lp = (1 - l) if q == 0 else l
        return remote(tok.at[:, lp], X.at[1, :, lp], tk_s.at[q], tk_r.at[q], partner)

    def tok_cross(p):
        return remote(tok.at[p, 1 - l], X.at[2, p, 1 - l], tk_s.at[2 + p], tk_r.at[2 + p], cross)

    def tok_cross_in(p):
        return remote(X.at[2, p, l], X.at[2, p, l], tk_s.at[2 + p], tk_r.at[2 + p], cross)

    def tok_relay(p):
        return remote(X.at[2, p, l], X.at[2, p, l], tk_s.at[6 + p], tk_r.at[6 + p], y_near)

    def tok_relay_in(p):
        return remote(X.at[2, p, 1 - l], X.at[2, p, 1 - l], tk_s.at[6 + p], tk_r.at[6 + p], y_near)

    def tok_forward(q, p):
        lp = l if q == 0 else 1 - l
        i = 10 + 4 * q + p
        return remote(X.at[2, p, lp], X.at[3, p, lp], tk_s.at[i], tk_r.at[i], partner)

    def tok_forward_in(q, p):
        lp = l if q == 0 else 1 - l
        i = 10 + 4 * q + p
        return remote(X.at[3, p, lp], X.at[3, p, lp], tk_s.at[i], tk_r.at[i], partner)

    go(tok_pair(0))
    for p in range(NX):
        go(tok_cross(p))
    go(tok_pair(1))

    def cross_piece(p):
        tok_cross_in(p).wait_recv()
        go(tok_relay(p))
        go(tok_forward(0, p))

    def relay_piece(p):
        tok_relay_in(p).wait_recv()
        go(tok_forward(1, p))

    def flatten(j):
        weight_copy(j).wait()
        depth = flat.shape[0] // 2

        def part(i, carry):
            k = pl.multiple_of(i * depth, depth)
            flat[...] = raw[j, pl.ds(k, depth)].reshape(2 * depth, LANES).astype(F32)
            W[j, pl.ds(k, depth), 0:LANES] = flat[pl.ds(0, depth, stride=2), :].astype(BF16)
            W[j, pl.ds(k, depth), LANES:] = flat[pl.ds(1, depth, stride=2), :].astype(BF16)
            return carry

        lax.fori_loop(0, W.shape[1] // depth, part, 0)

    def project(u, j0, j1):
        hb, lp = unit_half[u]

        def block(j, carry):
            if u == 0:
                flatten(j)
            rows = X[2 * hb:2 * hb + 2, :, lp].reshape(NZ * ROWS, X.shape[-1])
            sums = jnp.dot(rows, W[j], preferred_element_type=F32)
            columns = pl.ds(pl.multiple_of(j * 2 * LANES, 2 * LANES), 2 * LANES)
            PS[u, :, :, columns] = sums.reshape(NZ, ROWS, 2 * LANES)
            return carry

        lax.fori_loop(j0, j1, block, 0)

    def hops(g, d):
        return 4 if g == d else 3

    def slot(g, d, k):
        return k if g == d else 4 + k

    def z_copy(u, g, d, k):
        i = 7 * g + slot(g, d, k)
        ref = slot(g, d, k)
        return remote(
            sends[g].at[u, ref], receives[g].at[u, ref], rs_s.at[u, i], rs_r.at[u, i], z_next if d == 0 else z_prev
        )

    def step(d, k):
        return k if d == 0 else -k

    def sum_send(u, g, d, k):
        n = hops(g, d)
        o = lax.rem(z + step(d, n - k) + NZ, NZ)
        v = PS[u, o, :, first[g]:first[g] + wide[g]]
        if k > 0:
            z_copy(u, g, d, k - 1).wait_recv()
            v = v + decode(receives[g][u, slot(g, d, k - 1)])
        sends[g][u, slot(g, d, k)] = encode(v)
        go(z_copy(u, g, d, k))

    def sum_last(u, g):
        for d in (0, 1):
            z_copy(u, g, d, hops(g, d) - 1).wait_recv()
        v = PS[u, z, :, first[g]:first[g] + wide[g]]
        for d in (0, 1):
            v = v + decode(receives[g][u, slot(g, d, hops(g, d) - 1)])
        for b in range(wide[g] // (2 * LANES)):
            gate = v[:, 2 * b * LANES:(2 * b + 1) * LANES]
            up = v[:, (2 * b + 1) * LANES:(2 * b + 2) * LANES]
            hidden[g][u, z, :, b * LANES:(b + 1) * LANES] = (gate / (1 + jnp.exp(-gate)) * up).astype(BF16)

    def h_copy(u, g, d, k, o):
        i = 7 * g + slot(g, d, k)
        ref = hidden[g].at[u, o]
        return remote(ref, ref, ag_s.at[u, i], ag_r.at[u, i], z_next if d == 0 else z_prev)

    def h_wait(u, g, d, k):
        h_copy(u, g, d, k, lax.rem(z - step(d, k + 1) + NZ, NZ)).wait_recv()

    def h_send(u, g, d, k):
        if k > 0:
            h_wait(u, g, d, k - 1)
        go(h_copy(u, g, d, k, lax.rem(z - step(d, k) + NZ, NZ)))

    half = own.shape[-1]

    def pair_copy(u, b):
        return remote(pair_out.at[u, b], pair_in.at[u, b], pr_s.at[u, b], pr_r.at[u, b], partner)

    def project_down(u, b):
        ka = HA.shape[-1]

        def block(i, carry):
            at = pl.multiple_of(i * 2 * LANES, 2 * LANES)
            columns = pl.ds(b * half + at, 2 * LANES)
            v = jnp.dot(HA[u].reshape(NZ * ROWS, ka), D[0:ka, columns], preferred_element_type=F32)
            v = v + jnp.dot(
                HB[u].reshape(NZ * ROWS, HB.shape[-1]), D[ka:, columns], preferred_element_type=F32
            )
            v = v.reshape(2, NX, ROWS, 2 * LANES)
            own[u % 2, b, :, :, pl.ds(at, 2 * LANES)] = v[0]
            pair_out[u, b, :, :, pl.ds(at, 2 * LANES)] = v[1].astype(BF16)
            return carry

        lax.fori_loop(0, half // (2 * LANES), block, 0)
        go(pair_copy(u, b))

    def x_copy(u, i):
        return remote(xs.at[u, i], xr.at[u, i], x_s.at[u, i], x_r.at[u, i], x_next if i < 3 else x_prev)

    def piece(u, b, k):
        p = lax.rem(x + k + NX, NX)
        return own[u % 2, b, p] + pair_in[u, b, p].astype(F32)

    def x_first(u):
        for b in (0, 1):
            pair_copy(u, b).wait_recv()
            i = 3 * b
            xs[u, i] = piece(u, b, 2).astype(BF16)
            go(x_copy(u, i))
            i = 4 if b == 0 else 1
            xs[u, i] = piece(u, b, -1 if b == 0 else 1).astype(BF16)
            go(x_copy(u, i))

    def x_second(u):
        for b in (0, 1):
            i = 3 * b
            x_copy(u, i).wait_recv()
            xs[u, i + 2] = (piece(u, b, 1 if b == 0 else -1) + xr[u, i].astype(F32)).astype(BF16)
            go(x_copy(u, i + 2))

    def y_copy(u, b):
        return remote(ys.at[u, b], yr.at[u, b], y_s.at[u, b], y_r.at[u, b], unit_target[u])

    def x_last(u):
        for b in (0, 1):
            two, one = 3 * b + 2, (4 if b == 0 else 1)
            x_copy(u, one).wait_recv()
            x_copy(u, two).wait_recv()
            v = piece(u, b, 0) + xr[u, one].astype(F32) + xr[u, two].astype(F32)
            if u < UNITS - 1:
                ys[u, b] = v.astype(BF16)
                go(y_copy(u, b))
            else:
                for other in range(UNITS - 1):
                    y_copy(other, b).wait_recv()
                    v = v + yr[other, b].astype(F32)
                out[:, b * half:(b + 1) * half] = v.astype(BF16)

    order = ((0, 0), (1, 1), (0, 1), (1, 0))
    own_copy(0).wait()
    tok_pair(0).wait_recv()
    for tick in range(START[-1] + 12):
        for u in range(UNITS):
            k = tick - START[u]
            if k == 0:
                for g, j0, j1 in ((0, 0, blocks_a), (1, blocks_a, blocks)):
                    if u == 0:
                        project(u, j0, j1)
                    for d in (0, 1):
                        sum_send(u, g, d, 0)
        for u in range(UNITS):
            k = tick - START[u]
            if 5 <= k < 8:
                for g, d in order:
                    if k - 4 < hops(g, d):
                        h_send(u, g, d, k - 4)
            if 1 <= k < 4:
                for g, d in order:
                    if k < hops(g, d):
                        sum_send(u, g, d, k)
            if k == 4:
                for g in (0, 1):
                    sum_last(u, g)
                    for d in (0, 1):
                        h_send(u, g, d, 0)
            if k == 8:
                if u == 0:
                    down_copy.wait()
                for g, d in order:
                    h_wait(u, g, d, hops(g, d) - 1)
                for b in (0, 1):
                    project_down(u, b)
            if k == 9:
                x_first(u)
            if k == 10:
                x_second(u)
            if k == 11:
                x_last(u)
        if tick < 2:
            cross_piece(tick)
        elif tick == 2:
            cross_piece(2)
            cross_piece(3)
        elif tick == 3:
            for p in range(NX):
                tok_forward_in(0, p).wait_recv()
            project(1, 0, blocks)
            for p in range(NX):
                relay_piece(p)
        elif tick == 4:
            for p in range(NX):
                tok_forward_in(1, p).wait_recv()
        if 4 <= tick < 7:
            project(2, (0, 3, 5)[tick - 4], (3, 5, 7)[tick - 4])
        if tick == 7:
            own_copy(1).wait()
            tok_pair(1).wait_recv()
        if 7 <= tick < 10:
            project(3, (0, 3, 5)[tick - 7], (3, 5, 7)[tick - 7])

    for copy in started:
        copy.wait_send()


def shards(tokens, gate_up_weight, down_weight):
    width = tokens.shape[1]
    units = gate_up_weight.shape[2]
    blocks = units // LANES
    ua = (blocks + 1) // 2 * LANES
    ub = units - ua
    half = width // 2
    dma = pltpu.SemaphoreType.DMA
    any_space = pl.BlockSpec(memory_space=pl.ANY)
    vmem = pltpu.VMEM
    return pl.pallas_call(
        kernel,
        out_shape=jax.ShapeDtypeStruct((ROWS, width), BF16),
        in_specs=[any_space] * 3,
        out_specs=pl.BlockSpec(memory_space=pltpu.VMEM),
        scratch_shapes=[
            vmem((4, NX, 2, ROWS, width), BF16),
            vmem((blocks, width, 2, LANES), BF16),
            vmem((512, LANES), F32),
            vmem((blocks, width, 2 * LANES), BF16),
            vmem((units, width), BF16),
            vmem((UNITS, NZ, ROWS, 2 * units), F32),
            vmem((UNITS, 7, ROWS, 2 * ua), BF16),
            vmem((UNITS, 7, ROWS, 2 * ub), BF16),
            vmem((UNITS, 7, ROWS, 2 * ua), BF16),
            vmem((UNITS, 7, ROWS, 2 * ub), BF16),
            vmem((UNITS, NZ, ROWS, ua), BF16),
            vmem((UNITS, NZ, ROWS, ub), BF16),
            vmem((2, 2, NX, ROWS, half), F32),
            vmem((UNITS, 2, NX, ROWS, half), BF16),
            vmem((UNITS, 2, NX, ROWS, half), BF16),
            vmem((UNITS, 6, ROWS, half), BF16),
            vmem((UNITS, 6, ROWS, half), BF16),
            vmem((UNITS - 1, 2, ROWS, half), BF16),
            vmem((UNITS - 1, 2, ROWS, half), BF16),
            dma((3,)),
            dma((blocks,)),
            dma((18,)),
            dma((18,)),
            dma((UNITS, 14)),
            dma((UNITS, 14)),
            dma((UNITS, 14)),
            dma((UNITS, 14)),
            dma((UNITS, 2)),
            dma((UNITS, 2)),
            dma((UNITS, 6)),
            dma((UNITS, 6)),
            dma((UNITS - 1, 2)),
            dma((UNITS - 1, 2)),
        ],
        compiler_params=pltpu.CompilerParams(
            collective_id=0, has_side_effects=True, vmem_limit_bytes=62 << 20
        ),
    )(tokens.reshape(NX, 2, ROWS, width), gate_up_weight, down_weight)


def solution(mesh):
    placed = (P("inp", "out"), P("out", None, ("inp", "dep")), P(("inp", "dep"), "out"))
    return jax.shard_map(
        shards, mesh=mesh, in_specs=placed, out_specs=P(("inp", "dep"), "out"), check_vma=False
    )
```

```python
import jax
import jax.numpy as jnp
from jax import lax
from jax.experimental import pallas as pl
from jax.experimental.pallas import tpu as pltpu
from jax.sharding import PartitionSpec as P

MESH = pl.DeviceIdType.MESH
BF16, F32 = jnp.bfloat16, jnp.float32
UNITS, NZ, NX, ROWS = 4, 8, 4, 32
LANES = 128
GROUPS = (4, 3)
STAGES = ((0, 0, 32), (1, 0, 32), (2, 0, 32), (3, 0, 32))
PARTS = 4
LONG = ((False, False), (False, False), (False, False), (False, True))
CROSS, RELAY, WEIGHT, PRODUCT, SUM, END, HIDDEN, DOWN, X1, X2, X3 = range(11)
ORDER = (
    (WEIGHT, 0), (WEIGHT, 1), (WEIGHT, 2), (WEIGHT, 3), (PRODUCT, 3, 0), (PRODUCT, 3, 1), (PRODUCT, 3, 2), (PRODUCT, 3, 3),
    (SUM, 3, 0, 0, 0), (SUM, 3, 0, 1, 0), (PRODUCT, 0, 0), (PRODUCT, 0, 1), (PRODUCT, 0, 2), (PRODUCT, 0, 3),
    (SUM, 0, 0, 1, 0), (SUM, 0, 0, 0, 0), (WEIGHT, 4), (PRODUCT, 0, 4), (CROSS, 0), (CROSS, 1), (WEIGHT, 5),
    (SUM, 3, 0, 0, 1), (PRODUCT, 0, 5), (WEIGHT, 6), (PRODUCT, 0, 6), (SUM, 0, 1, 0, 0), (SUM, 0, 1, 1, 0),
    (SUM, 0, 0, 1, 1), (CROSS, 2), (SUM, 0, 0, 0, 1), (PRODUCT, 3, 4), (PRODUCT, 3, 5), (PRODUCT, 3, 6), (SUM, 3, 0, 1, 1),
    (SUM, 3, 1, 0, 0), (CROSS, 3), (SUM, 3, 1, 1, 0), (PRODUCT, 1, 0), (SUM, 3, 0, 0, 2), (PRODUCT, 1, 1), (PRODUCT, 1, 2),
    (PRODUCT, 1, 3), (SUM, 1, 0, 0, 0), (SUM, 0, 1, 1, 1), (SUM, 1, 0, 1, 0), (RELAY, 0), (RELAY, 1), (RELAY, 2),
    (SUM, 0, 0, 0, 2), (SUM, 0, 0, 1, 2), (SUM, 0, 1, 0, 1), (PRODUCT, 1, 4), (PRODUCT, 1, 5), (PRODUCT, 1, 6),
    (SUM, 1, 1, 1, 0), (SUM, 1, 1, 0, 0), (RELAY, 3), (SUM, 3, 1, 0, 1), (SUM, 3, 1, 1, 1), (PRODUCT, 2, 0),
    (PRODUCT, 2, 1), (SUM, 1, 0, 0, 1), (SUM, 0, 1, 1, 2), (PRODUCT, 2, 2), (SUM, 1, 0, 1, 1), (SUM, 0, 0, 0, 3),
    (PRODUCT, 2, 3), (SUM, 2, 0, 0, 0), (SUM, 0, 1, 0, 2), (SUM, 1, 1, 1, 1), (PRODUCT, 2, 4), (SUM, 2, 0, 1, 0),
    (SUM, 1, 1, 0, 1), (PRODUCT, 2, 5), (PRODUCT, 2, 6), (SUM, 2, 1, 1, 0), (SUM, 2, 1, 0, 0), (SUM, 1, 0, 0, 2),
    (SUM, 0, 1, 1, 3), (SUM, 1, 1, 1, 2), (END, 0, 0), (HIDDEN, 0, 0, 1, 0), (HIDDEN, 0, 0, 0, 0), (SUM, 2, 0, 0, 1),
    (SUM, 2, 0, 1, 1), (SUM, 2, 1, 1, 1), (SUM, 1, 1, 0, 2), (END, 0, 1), (HIDDEN, 0, 1, 1, 0), (SUM, 2, 1, 0, 1),
    (SUM, 1, 1, 1, 3), (SUM, 1, 0, 1, 2), (SUM, 1, 0, 0, 3), (SUM, 3, 1, 1, 2), (SUM, 2, 0, 0, 2), (HIDDEN, 0, 1, 0, 0),
    (SUM, 2, 1, 1, 2), (HIDDEN, 0, 1, 1, 1), (HIDDEN, 0, 0, 1, 1), (HIDDEN, 0, 0, 0, 1), (SUM, 2, 1, 0, 2), (END, 1, 1),
    (HIDDEN, 1, 1, 1, 0), (HIDDEN, 1, 1, 0, 0), (SUM, 2, 0, 1, 2), (END, 1, 0), (HIDDEN, 1, 0, 0, 0), (HIDDEN, 1, 0, 1, 0),
    (SUM, 2, 0, 0, 3), (SUM, 2, 1, 1, 3), (HIDDEN, 0, 1, 0, 1), (HIDDEN, 0, 0, 0, 2), (HIDDEN, 0, 1, 1, 2),
    (SUM, 3, 1, 0, 2), (HIDDEN, 1, 1, 1, 1), (SUM, 3, 0, 1, 2), (SUM, 3, 1, 1, 3), (HIDDEN, 1, 0, 0, 1), (SUM, 3, 0, 0, 3),
    (HIDDEN, 1, 0, 1, 1), (END, 2, 0), (HIDDEN, 2, 0, 0, 0), (HIDDEN, 1, 1, 0, 1), (END, 2, 1), (HIDDEN, 2, 1, 1, 0),
    (HIDDEN, 0, 1, 0, 2), (HIDDEN, 1, 1, 1, 2), (HIDDEN, 0, 1, 1, 3), (HIDDEN, 0, 0, 1, 2), (HIDDEN, 1, 0, 0, 2),
    (HIDDEN, 2, 0, 1, 0), (HIDDEN, 0, 0, 0, 3), (END, 3, 0), (HIDDEN, 2, 1, 0, 0), (HIDDEN, 2, 0, 0, 1),
    (HIDDEN, 3, 0, 0, 0), (HIDDEN, 2, 1, 1, 1), (HIDDEN, 1, 0, 1, 2), (HIDDEN, 1, 1, 0, 2), (HIDDEN, 1, 1, 1, 3),
    (END, 3, 1), (HIDDEN, 3, 1, 1, 1), (HIDDEN, 1, 0, 0, 3), (HIDDEN, 3, 1, 0, 1), (DOWN, 0, 0), (HIDDEN, 2, 1, 0, 1),
    (HIDDEN, 2, 0, 1, 1), (HIDDEN, 3, 1, 1, 0), (DOWN, 0, 1), (HIDDEN, 2, 0, 0, 2), (DOWN, 0, 2), (HIDDEN, 2, 1, 1, 2),
    (HIDDEN, 3, 0, 0, 1), (HIDDEN, 3, 0, 1, 1), (X1, 0, 0), (DOWN, 0, 3), (X1, 0, 1), (DOWN, 1, 0), (X1, 0, 2),
    (DOWN, 1, 1), (HIDDEN, 2, 1, 0, 2), (X1, 0, 3), (HIDDEN, 2, 0, 1, 2), (DOWN, 1, 2), (HIDDEN, 2, 0, 0, 3), (X1, 1, 0),
    (HIDDEN, 2, 1, 1, 3), (HIDDEN, 3, 1, 1, 3), (HIDDEN, 3, 0, 1, 0), (X2, 0, 0), (X1, 1, 1), (HIDDEN, 3, 0, 0, 2),
    (HIDDEN, 3, 1, 0, 0), (HIDDEN, 3, 1, 1, 2), (DOWN, 1, 3), (X2, 0, 1), (X1, 1, 2), (X2, 0, 2), (X2, 0, 3),
    (HIDDEN, 3, 1, 0, 2), (HIDDEN, 3, 0, 0, 3), (X1, 1, 3), (X2, 1, 0), (HIDDEN, 3, 0, 1, 2), (X3, 0, 0), (X2, 1, 1),
    (DOWN, 2, 0), (X3, 0, 1), (DOWN, 2, 1), (X2, 1, 2), (X3, 0, 2), (DOWN, 2, 2), (X1, 2, 0), (X3, 0, 3), (X2, 1, 3),
    (DOWN, 2, 3), (X1, 2, 1), (X3, 1, 0), (DOWN, 3, 0), (X1, 2, 2), (X3, 1, 1), (DOWN, 3, 1), (X1, 2, 3), (X3, 1, 2),
    (DOWN, 3, 2), (X1, 3, 0), (X2, 2, 0), (X3, 1, 3), (X1, 3, 1), (DOWN, 3, 3), (X2, 2, 1), (X1, 3, 2), (X2, 2, 2),
    (X2, 2, 3), (X1, 3, 3), (X2, 3, 1), (X3, 2, 1), (X2, 3, 0), (X3, 2, 0), (X3, 2, 2), (X2, 3, 2), (X3, 2, 3), (X2, 3, 3),
    (X3, 3, 1), (X3, 3, 0), (X3, 3, 2), (X3, 3, 3),
)


def encode(v):
    return (v * jnp.abs(v)).astype(BF16)


def decode(v):
    v = v.astype(F32)
    root = jnp.sqrt(jnp.abs(v))
    return jnp.where(v < 0, -root, root)


def kernel(
    tok, gate_up, down, out,
    X, raw, flat, W, D, PS, S, R, H, own, pair_out, pair_in, xs, xr, ys, yr,
    ld_sem, w_sem, tk_s, tk_r, rs_s, rs_r, ag_s, ag_r, pr_s, pr_r, x_s, x_r, y_s, y_r,
):
    inp, dep, z = lax.axis_index("inp"), lax.axis_index("dep"), lax.axis_index("out")
    x, l = dep // 2, lax.rem(dep, 2)
    h, c = inp // 2, lax.rem(inp, 2)
    dep_l = x * 2 + (1 - l)
    partner = (h * 2 + (1 - c), dep, z)
    y_near = (inp, dep_l, z)
    y_far = ((1 - h) * 2 + c, dep, z)
    cross = ((1 - h) * 2 + c, dep_l, z)
    x_side = ((inp, lax.rem(dep + 2, 8), z), (inp, lax.rem(dep + 6, 8), z))
    reach = 3 if any(a or b for a, b in LONG) else 1
    z_side = tuple((inp, dep, lax.rem(z + k, NZ)) for k in range(1, reach + 1))
    z_side += tuple((inp, dep, lax.rem(z + NZ - k, NZ)) for k in range(1, reach + 1))
    unit_half = ((0, 1 - l), (1, l), (1, 1 - l), (0, l))
    unit_target = (y_near, y_far, cross)
    blocks = raw.shape[0]
    first = [sum(GROUPS[:g]) for g in range(len(GROUPS))]
    part = own.shape[-1]
    started = []

    def weight_copy(j):
        columns = pl.ds(j * LANES, LANES)
        return pltpu.make_async_copy(gate_up.at[:, :, columns], raw.at[j], w_sem.at[j])

    def own_copy(q):
        lp = (1 - l) if q == 0 else l
        return pltpu.make_async_copy(tok.at[:, lp], X.at[0, :, lp], ld_sem.at[q])

    down_copy = pltpu.make_async_copy(down, D, ld_sem.at[2])

    def remote(src, dst, s, r, device):
        return pltpu.make_async_remote_copy(
            src_ref=src, dst_ref=dst, send_sem=s, recv_sem=r, device_id=device, device_id_type=MESH
        )

    def go(copy):
        copy.start()
        started.append(copy)

    own_copy(0).start()
    for j in range(blocks):
        weight_copy(j).start()
    own_copy(1).start()
    down_copy.start()

    barrier = pltpu.get_barrier_semaphore()
    peers = (partner, y_near, y_far, cross) + x_side + z_side
    for peer in peers:
        pl.semaphore_signal(barrier, inc=1, device_id=peer, device_id_type=MESH)
    pl.semaphore_wait(barrier, len(peers))

    def tok_pair(q):
        lp = (1 - l) if q == 0 else l
        return remote(tok.at[:, lp], X.at[1, :, lp], tk_s.at[q], tk_r.at[q], partner)

    def tok_cross(p):
        return remote(tok.at[p, 1 - l], X.at[2, p, 1 - l], tk_s.at[2 + p], tk_r.at[2 + p], cross)

    def tok_cross_in(p):
        return remote(X.at[2, p, l], X.at[2, p, l], tk_s.at[2 + p], tk_r.at[2 + p], cross)

    def tok_relay(p):
        return remote(X.at[2, p, l], X.at[2, p, l], tk_s.at[6 + p], tk_r.at[6 + p], y_near)

    def tok_relay_in(p):
        return remote(X.at[2, p, 1 - l], X.at[2, p, 1 - l], tk_s.at[6 + p], tk_r.at[6 + p], y_near)

    def tok_forward(q, p):
        lp = l if q == 0 else 1 - l
        i = 10 + 4 * q + p
        return remote(X.at[2, p, lp], X.at[3, p, lp], tk_s.at[i], tk_r.at[i], partner)

    def tok_forward_in(q, p):
        lp = l if q == 0 else 1 - l
        i = 10 + 4 * q + p
        return remote(X.at[3, p, lp], X.at[3, p, lp], tk_s.at[i], tk_r.at[i], partner)

    go(tok_pair(0))
    for p in range(NX):
        go(tok_cross(p))
    go(tok_pair(1))

    def cross_piece(p):
        tok_cross_in(p).wait_recv()
        go(tok_forward(0, p))
        go(tok_relay(p))

    def relay_piece(p):
        tok_relay_in(p).wait_recv()
        go(tok_forward(1, p))

    def rows_ready(u):
        if u in (0, 3):
            q = 0 if u == 0 else 1
            own_copy(q).wait()
            tok_pair(q).wait_recv()
        else:
            for p in range(NX):
                tok_forward_in(u - 1, p).wait_recv()

    def flatten(j):
        weight_copy(j).wait()
        depth = flat.shape[0] // 2

        def piece(i, carry):
            k = pl.multiple_of(i * depth, depth)
            flat[...] = raw[j, pl.ds(k, depth)].reshape(2 * depth, LANES).astype(F32)
            W[j, pl.ds(k, depth), 0:LANES] = flat[pl.ds(0, depth, stride=2), :].astype(BF16)
            W[j, pl.ds(k, depth), LANES:] = flat[pl.ds(1, depth, stride=2), :].astype(BF16)
            return carry

        lax.fori_loop(0, W.shape[1] // depth, piece, 0)

    def project(u, j0, j1):
        hb, lp = unit_half[u]

        def block(j, carry):
            rows = X[2 * hb:2 * hb + 2, :, lp].reshape(NZ * ROWS, X.shape[-1])
            sums = jnp.dot(rows, W[j], preferred_element_type=F32)
            columns = pl.ds(pl.multiple_of(j * 2 * LANES, 2 * LANES), 2 * LANES)
            PS[u, :, :, columns] = sums.reshape(NZ, ROWS, 2 * LANES)
            return carry

        lax.fori_loop(j0, j1, block, 0)

    def hops(g, d):
        return 4 if g % 2 == d else 3

    def slot(g, d, k):
        return k if g % 2 == d else 4 + k

    def step(d, k):
        return k if d == 0 else -k

    def around(d, k):
        return lax.rem(z + step(d, k) + NZ, NZ)

    def sum_table(v, g, d):
        n = hops(g, d)
        if not LONG[v][0]:
            return [(n - k, k - 1 if k else None, 1) for k in range(n)]
        if n == 4:
            return [(4, None, 1), (2, None, 1), (3, 0, 3), (1, 1, 1)]
        return [(3, None, 1), (1, None, 1), (2, 0, 2)]

    def hidden_table(v, g, d):
        n = hops(g, d)
        if not LONG[v][1]:
            return [(k, k - 1 if k else None, 1) for k in range(n)]
        if n == 4:
            return [(0, None, 1), (0, None, 3), (1, 0, 1), (3, 1, 1)]
        return [(0, None, 1), (0, None, 2), (2, 1, 1)]

    def z_peer(d, far):
        return (inp, dep, around(d, far))

    def sums_at(v, g):
        u, r0, r1 = STAGES[v]
        lo = first[g] * 2 * LANES
        return u, slice(r0, r1), slice(lo, lo + GROUPS[g] * 2 * LANES)

    def z_copy(v, g, d, k):
        u, rows, columns = sums_at(v, g)
        i = 7 * g + slot(g, d, k)
        at = (u, slot(g, d, k), rows, columns)
        return remote(S.at[at], R.at[at], rs_s.at[v, i], rs_r.at[v, i], z_peer(d, sum_table(v, g, d)[k][2]))

    def sum_send(v, g, d, k):
        u, rows, columns = sums_at(v, g)
        owner, after, far = sum_table(v, g, d)[k]
        t = PS[u, around(d, owner), rows, columns]
        if after is not None:
            z_copy(v, g, d, after).wait_recv()
            t = t + decode(R[u, slot(g, d, after), rows, columns])
        S[u, slot(g, d, k), rows, columns] = encode(t)
        go(z_copy(v, g, d, k))

    def sum_last(v, g):
        u, rows, columns = sums_at(v, g)
        t = PS[u, z, rows, columns]
        for d in (0, 1):
            for k, (owner, after, far) in enumerate(sum_table(v, g, d)):
                if owner == far:
                    z_copy(v, g, d, k).wait_recv()
                    t = t + decode(R[u, slot(g, d, k), rows, columns])
        for b in range(GROUPS[g]):
            gate = t[:, 2 * b * LANES:(2 * b + 1) * LANES]
            up = t[:, (2 * b + 1) * LANES:(2 * b + 2) * LANES]
            lo = (first[g] + b) * LANES
            H[u, z, rows, lo:lo + LANES] = (gate / (1 + jnp.exp(-gate)) * up).astype(BF16)

    def h_copy(v, g, d, k, o):
        u, r0, r1 = STAGES[v]
        i = 7 * g + slot(g, d, k)
        ref = H.at[u, o, r0:r1, first[g] * LANES:(first[g] + GROUPS[g]) * LANES]
        return remote(ref, ref, ag_s.at[v, i], ag_r.at[v, i], z_peer(d, hidden_table(v, g, d)[k][2]))

    def h_wait(v, g, d, k):
        origin, after, far = hidden_table(v, g, d)[k]
        h_copy(v, g, d, k, around(d, -(origin + far))).wait_recv()

    def h_send(v, g, d, k):
        origin, after, far = hidden_table(v, g, d)[k]
        if after is not None:
            h_wait(v, g, d, after)
        go(h_copy(v, g, d, k, around(d, -origin)))

    def pair_copy(v, b):
        u, r0, r1 = STAGES[v]
        at = (u, b, slice(None), slice(r0, r1))
        return remote(pair_out.at[at], pair_in.at[at], pr_s.at[v, b], pr_r.at[v, b], partner)

    def project_down(v, b):
        u, r0, r1 = STAGES[v]
        if b == 0:
            for g in range(len(GROUPS)):
                for d in (0, 1):
                    for k in range(hops(g, d)):
                        if all(after != k for origin, after, far in hidden_table(v, g, d)):
                            h_wait(v, g, d, k)

        def block(i, carry):
            at = pl.multiple_of(i * 2 * LANES, 2 * LANES)
            rows = H[u, :, r0:r1, :].reshape(NZ * (r1 - r0), H.shape[-1])
            t = jnp.dot(rows, D[:, pl.ds(b * part + at, 2 * LANES)], preferred_element_type=F32)
            t = t.reshape(2, NX, r1 - r0, 2 * LANES)
            own[v % 2, b, :, r0:r1, pl.ds(at, 2 * LANES)] = t[0]
            pair_out[u, b, :, r0:r1, pl.ds(at, 2 * LANES)] = t[1].astype(BF16)
            return carry

        lax.fori_loop(0, part // (2 * LANES), block, 0)
        go(pair_copy(v, b))

    def x_copy(v, b, i):
        u, r0, r1 = STAGES[v]
        d = b % 2 if i != 1 else 1 - b % 2
        at = (u, 3 * b + i, slice(r0, r1))
        return remote(xs.at[at], xr.at[at], x_s.at[v, 3 * b + i], x_r.at[v, 3 * b + i], x_side[d])

    def piece(v, b, k):
        u, r0, r1 = STAGES[v]
        p = lax.rem(x + k + NX, NX)
        return own[v % 2, b, p, r0:r1] + pair_in[u, b, p, r0:r1].astype(F32)

    def x_first(v, b):
        u, r0, r1 = STAGES[v]
        pair_copy(v, b).wait_recv()
        for i, k in ((0, 2), (1, step(b % 2, -1))):
            xs[u, 3 * b + i, r0:r1] = piece(v, b, k).astype(BF16)
            go(x_copy(v, b, i))

    def x_second(v, b):
        u, r0, r1 = STAGES[v]
        x_copy(v, b, 0).wait_recv()
        t = piece(v, b, step(b % 2, 1)) + xr[u, 3 * b, r0:r1].astype(F32)
        xs[u, 3 * b + 2, r0:r1] = t.astype(BF16)
        go(x_copy(v, b, 2))

    def y_copy(v, b):
        u, r0, r1 = STAGES[v]
        return remote(
            ys.at[u, b, r0:r1], yr.at[u, b, r0:r1], y_s.at[v, b], y_r.at[v, b], unit_target[u]
        )

    arrived = set()

    def x_last(v, b):
        u, r0, r1 = STAGES[v]
        t = piece(v, b, 0)
        for i in (1, 2):
            x_copy(v, b, i).wait_recv()
            t = t + xr[u, 3 * b + i, r0:r1].astype(F32)
        if u < UNITS - 1:
            ys[u, b, r0:r1] = t.astype(BF16)
            go(y_copy(v, b))
            return
        if b not in arrived:
            arrived.add(b)
            for other in range(len(STAGES)):
                if STAGES[other][0] < UNITS - 1:
                    y_copy(other, b).wait_recv()
        for other in range(UNITS - 1):
            t = t + yr[other, b, r0:r1].astype(F32)
        out[r0:r1, b * part:(b + 1) * part] = t.astype(BF16)

    steps = {
        CROSS: cross_piece, RELAY: relay_piece, WEIGHT: flatten, SUM: sum_send, END: sum_last, HIDDEN: h_send,
        DOWN: project_down, X1: x_first, X2: x_second, X3: x_last,
    }
    ready, fetched, i = set(), False, 0
    while i < len(ORDER):
        kind, *at = ORDER[i]
        i += 1
        if kind == PRODUCT:
            u, j = at
            if u not in ready:
                ready.add(u)
                rows_ready(u)
            end = j + 1
            while i < len(ORDER) and ORDER[i] == (PRODUCT, u, end):
                end, i = end + 1, i + 1
            project(u, j, end)
            continue
        if kind == DOWN and not fetched:
            fetched = True
            down_copy.wait()
        steps[kind](*at)

    for copy in started:
        copy.wait_send()


def shards(tokens, gate_up_weight, down_weight):
    width = tokens.shape[1]
    units = gate_up_weight.shape[2]
    blocks = units // LANES
    part = width // PARTS
    stages, links = len(STAGES), 7 * len(GROUPS)
    dma = pltpu.SemaphoreType.DMA
    any_space = pl.BlockSpec(memory_space=pl.ANY)
    vmem = pltpu.VMEM
    return pl.pallas_call(
        kernel,
        out_shape=jax.ShapeDtypeStruct((ROWS, width), BF16),
        in_specs=[any_space] * 3,
        out_specs=pl.BlockSpec(memory_space=pltpu.VMEM),
        scratch_shapes=[
            vmem((4, NX, 2, ROWS, width), BF16),
            vmem((blocks, width, 2, LANES), BF16),
            vmem((512, LANES), F32),
            vmem((blocks, width, 2 * LANES), BF16),
            vmem((units, width), BF16),
            vmem((UNITS, NZ, ROWS, 2 * units), F32),
            vmem((UNITS, 7, ROWS, 2 * units), BF16),
            vmem((UNITS, 7, ROWS, 2 * units), BF16),
            vmem((UNITS, NZ, ROWS, units), BF16),
            vmem((2, PARTS, NX, ROWS, part), F32),
            vmem((UNITS, PARTS, NX, ROWS, part), BF16),
            vmem((UNITS, PARTS, NX, ROWS, part), BF16),
            vmem((UNITS, 3 * PARTS, ROWS, part), BF16),
            vmem((UNITS, 3 * PARTS, ROWS, part), BF16),
            vmem((UNITS - 1, PARTS, ROWS, part), BF16),
            vmem((UNITS - 1, PARTS, ROWS, part), BF16),
            dma((3,)),
            dma((blocks,)),
            dma((18,)),
            dma((18,)),
            dma((stages, links)),
            dma((stages, links)),
            dma((stages, links)),
            dma((stages, links)),
            dma((stages, PARTS)),
            dma((stages, PARTS)),
            dma((stages, 3 * PARTS)),
            dma((stages, 3 * PARTS)),
            dma((stages, PARTS)),
            dma((stages, PARTS)),
        ],
        compiler_params=pltpu.CompilerParams(
            collective_id=0, has_side_effects=True, vmem_limit_bytes=62 << 20
        ),
    )(tokens.reshape(NX, 2, ROWS, width), gate_up_weight, down_weight)


def solution(mesh):
    placed = (P("inp", "out"), P("out", None, ("inp", "dep")), P(("inp", "dep"), "out"))
    return jax.shard_map(
        shards, mesh=mesh, in_specs=placed, out_specs=P(("inp", "dep"), "out"), check_vma=False
    )
```

```python
import jax
import jax.numpy as jnp
from jax import lax
from jax.experimental import pallas as pl
from jax.experimental.pallas import tpu as pltpu
from jax.sharding import PartitionSpec as P

MESH = pl.DeviceIdType.MESH
BF16, F32 = jnp.bfloat16, jnp.float32
UNITS, NZ, NX, ROWS = 4, 8, 4, 32
LANES = 128
GROUPS = (4, 3)
STAGES = ((0, 0, 32), (1, 0, 32), (2, 0, 32), (3, 0, 32))
PARTS = 4
LONG = ((False, False), (False, False), (False, False), (False, True))
CROSS, RELAY, WEIGHT, PRODUCT, SUM, END, HIDDEN, DOWN, X1, X2, X3 = range(11)
AHEAD = 2
ORDER = (
    (WEIGHT, 0), (WEIGHT, 1), (WEIGHT, 2), (WEIGHT, 3), (PRODUCT, 3, 0), (PRODUCT, 3, 1), (PRODUCT, 3, 2), (PRODUCT, 3, 3),
    (SUM, 3, 0, 0, 0), (SUM, 3, 0, 1, 0), (PRODUCT, 0, 0), (PRODUCT, 0, 1), (PRODUCT, 0, 2), (PRODUCT, 0, 3),
    (SUM, 0, 0, 1, 0), (SUM, 0, 0, 0, 0), (WEIGHT, 4), (PRODUCT, 0, 4), (CROSS, 0), (CROSS, 1), (WEIGHT, 5),
    (SUM, 3, 0, 0, 1), (PRODUCT, 0, 5), (WEIGHT, 6), (PRODUCT, 0, 6), (SUM, 0, 1, 0, 0), (SUM, 0, 1, 1, 0),
    (SUM, 0, 0, 1, 1), (CROSS, 2), (SUM, 0, 0, 0, 1), (PRODUCT, 3, 4), (PRODUCT, 3, 5), (PRODUCT, 3, 6), (SUM, 3, 0, 1, 1),
    (SUM, 3, 1, 0, 0), (CROSS, 3), (SUM, 3, 1, 1, 0), (PRODUCT, 1, 0), (SUM, 3, 0, 0, 2), (PRODUCT, 1, 1), (PRODUCT, 1, 2),
    (PRODUCT, 1, 3), (SUM, 1, 0, 0, 0), (SUM, 0, 1, 1, 1), (SUM, 1, 0, 1, 0), (RELAY, 0), (RELAY, 1), (RELAY, 2),
    (SUM, 0, 0, 0, 2), (SUM, 0, 0, 1, 2), (SUM, 0, 1, 0, 1), (PRODUCT, 1, 4), (PRODUCT, 1, 5), (PRODUCT, 1, 6),
    (SUM, 1, 1, 1, 0), (SUM, 1, 1, 0, 0), (RELAY, 3), (SUM, 3, 1, 0, 1), (SUM, 3, 1, 1, 1), (PRODUCT, 2, 0),
    (PRODUCT, 2, 1), (SUM, 1, 0, 0, 1), (SUM, 0, 1, 1, 2), (PRODUCT, 2, 2), (SUM, 1, 0, 1, 1), (SUM, 0, 0, 0, 3),
    (PRODUCT, 2, 3), (SUM, 2, 0, 0, 0), (SUM, 0, 1, 0, 2), (SUM, 1, 1, 1, 1), (PRODUCT, 2, 4), (SUM, 2, 0, 1, 0),
    (SUM, 1, 1, 0, 1), (PRODUCT, 2, 5), (PRODUCT, 2, 6), (SUM, 2, 1, 1, 0), (SUM, 2, 1, 0, 0), (SUM, 1, 0, 0, 2),
    (SUM, 0, 1, 1, 3), (SUM, 1, 1, 1, 2), (END, 0, 0), (HIDDEN, 0, 0, 1, 0), (HIDDEN, 0, 0, 0, 0), (SUM, 2, 0, 0, 1),
    (SUM, 2, 0, 1, 1), (SUM, 2, 1, 1, 1), (SUM, 1, 1, 0, 2), (END, 0, 1), (HIDDEN, 0, 1, 1, 0), (SUM, 2, 1, 0, 1),
    (SUM, 1, 1, 1, 3), (SUM, 1, 0, 1, 2), (SUM, 1, 0, 0, 3), (SUM, 3, 1, 1, 2), (SUM, 2, 0, 0, 2), (HIDDEN, 0, 1, 0, 0),
    (SUM, 2, 1, 1, 2), (HIDDEN, 0, 1, 1, 1), (HIDDEN, 0, 0, 1, 1), (HIDDEN, 0, 0, 0, 1), (SUM, 2, 1, 0, 2), (END, 1, 1),
    (HIDDEN, 1, 1, 1, 0), (HIDDEN, 1, 1, 0, 0), (SUM, 2, 0, 1, 2), (END, 1, 0), (HIDDEN, 1, 0, 0, 0), (HIDDEN, 1, 0, 1, 0),
    (SUM, 2, 0, 0, 3), (SUM, 2, 1, 1, 3), (HIDDEN, 0, 1, 0, 1), (HIDDEN, 0, 0, 0, 2), (HIDDEN, 0, 1, 1, 2),
    (SUM, 3, 1, 0, 2), (HIDDEN, 1, 1, 1, 1), (SUM, 3, 0, 1, 2), (SUM, 3, 1, 1, 3), (HIDDEN, 1, 0, 0, 1), (SUM, 3, 0, 0, 3),
    (HIDDEN, 1, 0, 1, 1), (END, 2, 0), (HIDDEN, 2, 0, 0, 0), (HIDDEN, 1, 1, 0, 1), (END, 2, 1), (HIDDEN, 2, 1, 1, 0),
    (HIDDEN, 0, 1, 0, 2), (HIDDEN, 1, 1, 1, 2), (HIDDEN, 0, 1, 1, 3), (HIDDEN, 0, 0, 1, 2), (HIDDEN, 1, 0, 0, 2),
    (HIDDEN, 2, 0, 1, 0), (HIDDEN, 0, 0, 0, 3), (END, 3, 0), (HIDDEN, 2, 1, 0, 0), (HIDDEN, 2, 0, 0, 1),
    (HIDDEN, 3, 0, 0, 0), (HIDDEN, 2, 1, 1, 1), (HIDDEN, 1, 0, 1, 2), (HIDDEN, 1, 1, 0, 2), (HIDDEN, 1, 1, 1, 3),
    (END, 3, 1), (HIDDEN, 3, 1, 1, 1), (HIDDEN, 1, 0, 0, 3), (HIDDEN, 3, 1, 0, 1), (DOWN, 0, 0), (HIDDEN, 2, 1, 0, 1),
    (HIDDEN, 2, 0, 1, 1), (HIDDEN, 3, 1, 1, 0), (DOWN, 0, 1), (HIDDEN, 2, 0, 0, 2), (DOWN, 0, 2), (HIDDEN, 2, 1, 1, 2),
    (HIDDEN, 3, 0, 0, 1), (HIDDEN, 3, 0, 1, 1), (X1, 0, 0), (DOWN, 0, 3), (X1, 0, 1), (DOWN, 1, 0), (X1, 0, 2),
    (DOWN, 1, 1), (HIDDEN, 2, 1, 0, 2), (X1, 0, 3), (HIDDEN, 2, 0, 1, 2), (DOWN, 1, 2), (HIDDEN, 2, 0, 0, 3), (X1, 1, 0),
    (HIDDEN, 2, 1, 1, 3), (HIDDEN, 3, 1, 1, 3), (HIDDEN, 3, 0, 1, 0), (X2, 0, 0), (X1, 1, 1), (HIDDEN, 3, 0, 0, 2),
    (HIDDEN, 3, 1, 0, 0), (HIDDEN, 3, 1, 1, 2), (DOWN, 1, 3), (X2, 0, 1), (X1, 1, 2), (X2, 0, 2), (X2, 0, 3),
    (HIDDEN, 3, 1, 0, 2), (HIDDEN, 3, 0, 0, 3), (X1, 1, 3), (X2, 1, 0), (HIDDEN, 3, 0, 1, 2), (X3, 0, 0), (X2, 1, 1),
    (DOWN, 2, 0), (X3, 0, 1), (DOWN, 2, 1), (X2, 1, 2), (X3, 0, 2), (DOWN, 2, 2), (X1, 2, 0), (X3, 0, 3), (X2, 1, 3),
    (DOWN, 2, 3), (X1, 2, 1), (X3, 1, 0), (DOWN, 3, 0), (X1, 2, 2), (X3, 1, 1), (DOWN, 3, 1), (X1, 2, 3), (X3, 1, 2),
    (DOWN, 3, 2), (X1, 3, 0), (X2, 2, 0), (X3, 1, 3), (X1, 3, 1), (DOWN, 3, 3), (X2, 2, 1), (X1, 3, 2), (X2, 2, 2),
    (X2, 2, 3), (X1, 3, 3), (X2, 3, 1), (X3, 2, 1), (X2, 3, 0), (X3, 2, 0), (X3, 2, 2), (X2, 3, 2), (X3, 2, 3), (X2, 3, 3),
    (X3, 3, 1), (X3, 3, 0), (X3, 3, 2), (X3, 3, 3),
)


def encode(v):
    return (v * jnp.abs(v)).astype(BF16)


def decode(v):
    v = v.astype(F32)
    root = jnp.sqrt(jnp.abs(v))
    return jnp.where(v < 0, -root, root)


def kernel(
    tok, gate_up, down, out,
    X, raw, flat, W, D, PS, S, R, H, own, pair_out, pair_in, xs, xr, ys, yr,
    ld_sem, w_sem, tk_s, tk_r, rs_s, rs_r, ag_s, ag_r, pr_s, pr_r, x_s, x_r, y_s, y_r,
):
    inp, dep, z = lax.axis_index("inp"), lax.axis_index("dep"), lax.axis_index("out")
    x, l = dep // 2, lax.rem(dep, 2)
    h, c = inp // 2, lax.rem(inp, 2)
    dep_l = x * 2 + (1 - l)
    partner = (h * 2 + (1 - c), dep, z)
    y_near = (inp, dep_l, z)
    y_far = ((1 - h) * 2 + c, dep, z)
    cross = ((1 - h) * 2 + c, dep_l, z)
    x_side = ((inp, lax.rem(dep + 2, 8), z), (inp, lax.rem(dep + 6, 8), z))
    reach = 3 if any(a or b for a, b in LONG) else 1
    z_side = tuple((inp, dep, lax.rem(z + k, NZ)) for k in range(1, reach + 1))
    z_side += tuple((inp, dep, lax.rem(z + NZ - k, NZ)) for k in range(1, reach + 1))
    unit_half = ((0, 1 - l), (1, l), (1, 1 - l), (0, l))
    unit_target = (y_near, y_far, cross)
    blocks = raw.shape[0]
    first = [sum(GROUPS[:g]) for g in range(len(GROUPS))]
    part = own.shape[-1]
    started = []

    def weight_copy(j):
        columns = pl.ds(j * LANES, LANES)
        return pltpu.make_async_copy(gate_up.at[:, :, columns], raw.at[j], w_sem.at[j])

    def own_copy(q):
        lp = (1 - l) if q == 0 else l
        return pltpu.make_async_copy(tok.at[:, lp], X.at[0, :, lp], ld_sem.at[q])

    down_copy = pltpu.make_async_copy(down, D, ld_sem.at[2])

    def remote(src, dst, s, r, device):
        return pltpu.make_async_remote_copy(
            src_ref=src, dst_ref=dst, send_sem=s, recv_sem=r, device_id=device, device_id_type=MESH
        )

    def go(copy):
        copy.start()
        started.append(copy)

    for j in range(blocks):
        weight_copy(j).start()
        if j < 2:
            own_copy(1 - j).start()
    down_copy.start()

    barrier = pltpu.get_barrier_semaphore()
    peers = (partner, y_near, y_far, cross) + x_side + z_side
    for peer in peers:
        pl.semaphore_signal(barrier, inc=1, device_id=peer, device_id_type=MESH)

    def tok_pair(q):
        lp = (1 - l) if q == 0 else l
        return remote(tok.at[:, lp], X.at[1, :, lp], tk_s.at[q], tk_r.at[q], partner)

    def tok_cross(p):
        return remote(tok.at[p, 1 - l], X.at[2, p, 1 - l], tk_s.at[2 + p], tk_r.at[2 + p], cross)

    def tok_cross_in(p):
        return remote(X.at[2, p, l], X.at[2, p, l], tk_s.at[2 + p], tk_r.at[2 + p], cross)

    def tok_relay(p):
        return remote(X.at[2, p, l], X.at[2, p, l], tk_s.at[6 + p], tk_r.at[6 + p], y_near)

    def tok_relay_in(p):
        return remote(X.at[2, p, 1 - l], X.at[2, p, 1 - l], tk_s.at[6 + p], tk_r.at[6 + p], y_near)

    def tok_forward(q, p):
        lp = l if q == 0 else 1 - l
        i = 10 + 4 * q + p
        return remote(X.at[2, p, lp], X.at[3, p, lp], tk_s.at[i], tk_r.at[i], partner)

    def tok_forward_in(q, p):
        lp = l if q == 0 else 1 - l
        i = 10 + 4 * q + p
        return remote(X.at[3, p, lp], X.at[3, p, lp], tk_s.at[i], tk_r.at[i], partner)

    def cross_piece(p):
        tok_cross_in(p).wait_recv()
        go(tok_forward(0, p))
        go(tok_relay(p))

    def relay_piece(p):
        tok_relay_in(p).wait_recv()
        go(tok_forward(1, p))

    def rows_ready(u):
        if u in (0, 3):
            q = 0 if u == 0 else 1
            own_copy(q).wait()
            tok_pair(q).wait_recv()
        else:
            for p in range(NX):
                tok_forward_in(u - 1, p).wait_recv()

    def flatten(j):
        weight_copy(j).wait()
        depth = flat.shape[0] // 2

        def piece(i, carry):
            k = pl.multiple_of(i * depth, depth)
            flat[...] = raw[j, pl.ds(k, depth)].reshape(2 * depth, LANES).astype(F32)
            W[j, pl.ds(k, depth), 0:LANES] = flat[pl.ds(0, depth, stride=2), :].astype(BF16)
            W[j, pl.ds(k, depth), LANES:] = flat[pl.ds(1, depth, stride=2), :].astype(BF16)
            return carry

        lax.fori_loop(0, W.shape[1] // depth, piece, 0)

    early = [at[0] for kind, *at in ORDER[:AHEAD]]
    for j in early:
        flatten(j)
    pl.semaphore_wait(barrier, len(peers))
    for p in range(NX):
        go(tok_cross(p))
    for q in (1, 0):
        go(tok_pair(q))

    def project(u, j0, j1):
        hb, lp = unit_half[u]

        def block(j, carry):
            rows = X[2 * hb:2 * hb + 2, :, lp].reshape(NZ * ROWS, X.shape[-1])
            sums = jnp.dot(rows, W[j], preferred_element_type=F32)
            columns = pl.ds(pl.multiple_of(j * 2 * LANES, 2 * LANES), 2 * LANES)
            PS[u, :, :, columns] = sums.reshape(NZ, ROWS, 2 * LANES)
            return carry

        lax.fori_loop(j0, j1, block, 0)

    def hops(g, d):
        return 4 if g % 2 == d else 3

    def slot(g, d, k):
        return k if g % 2 == d else 4 + k

    def step(d, k):
        return k if d == 0 else -k

    def around(d, k):
        return lax.rem(z + step(d, k) + NZ, NZ)

    def sum_table(v, g, d):
        n = hops(g, d)
        if not LONG[v][0]:
            return [(n - k, k - 1 if k else None, 1) for k in range(n)]
        if n == 4:
            return [(4, None, 1), (2, None, 1), (3, 0, 3), (1, 1, 1)]
        return [(3, None, 1), (1, None, 1), (2, 0, 2)]

    def hidden_table(v, g, d):
        n = hops(g, d)
        if not LONG[v][1]:
            return [(k, k - 1 if k else None, 1) for k in range(n)]
        if n == 4:
            return [(0, None, 1), (0, None, 3), (1, 0, 1), (3, 1, 1)]
        return [(0, None, 1), (0, None, 2), (2, 1, 1)]

    def z_peer(d, far):
        return (inp, dep, around(d, far))

    def sums_at(v, g):
        u, r0, r1 = STAGES[v]
        lo = first[g] * 2 * LANES
        return u, slice(r0, r1), slice(lo, lo + GROUPS[g] * 2 * LANES)

    def z_copy(v, g, d, k):
        u, rows, columns = sums_at(v, g)
        i = 7 * g + slot(g, d, k)
        at = (u, slot(g, d, k), rows, columns)
        return remote(S.at[at], R.at[at], rs_s.at[v, i], rs_r.at[v, i], z_peer(d, sum_table(v, g, d)[k][2]))

    def sum_send(v, g, d, k):
        u, rows, columns = sums_at(v, g)
        owner, after, far = sum_table(v, g, d)[k]
        t = PS[u, around(d, owner), rows, columns]
        if after is not None:
            z_copy(v, g, d, after).wait_recv()
            t = t + decode(R[u, slot(g, d, after), rows, columns])
        S[u, slot(g, d, k), rows, columns] = encode(t)
        go(z_copy(v, g, d, k))

    def sum_last(v, g):
        u, rows, columns = sums_at(v, g)
        t = PS[u, z, rows, columns]
        for d in (0, 1):
            for k, (owner, after, far) in enumerate(sum_table(v, g, d)):
                if owner == far:
                    z_copy(v, g, d, k).wait_recv()
                    t = t + decode(R[u, slot(g, d, k), rows, columns])
        for b in range(GROUPS[g]):
            gate = t[:, 2 * b * LANES:(2 * b + 1) * LANES]
            up = t[:, (2 * b + 1) * LANES:(2 * b + 2) * LANES]
            lo = (first[g] + b) * LANES
            H[u, z, rows, lo:lo + LANES] = (gate / (1 + jnp.exp(-gate)) * up).astype(BF16)

    def h_copy(v, g, d, k, o):
        u, r0, r1 = STAGES[v]
        i = 7 * g + slot(g, d, k)
        ref = H.at[u, o, r0:r1, first[g] * LANES:(first[g] + GROUPS[g]) * LANES]
        return remote(ref, ref, ag_s.at[v, i], ag_r.at[v, i], z_peer(d, hidden_table(v, g, d)[k][2]))

    def h_wait(v, g, d, k):
        origin, after, far = hidden_table(v, g, d)[k]
        h_copy(v, g, d, k, around(d, -(origin + far))).wait_recv()

    def h_send(v, g, d, k):
        origin, after, far = hidden_table(v, g, d)[k]
        if after is not None:
            h_wait(v, g, d, after)
        go(h_copy(v, g, d, k, around(d, -origin)))

    def pair_copy(v, b):
        u, r0, r1 = STAGES[v]
        at = (u, b, slice(None), slice(r0, r1))
        return remote(pair_out.at[at], pair_in.at[at], pr_s.at[v, b], pr_r.at[v, b], partner)

    def project_down(v, b):
        u, r0, r1 = STAGES[v]
        if b == 0:
            for g in range(len(GROUPS)):
                for d in (0, 1):
                    for k in range(hops(g, d)):
                        if all(after != k for origin, after, far in hidden_table(v, g, d)):
                            h_wait(v, g, d, k)

        def block(i, carry):
            at = pl.multiple_of(i * 2 * LANES, 2 * LANES)
            rows = H[u, :, r0:r1, :].reshape(NZ * (r1 - r0), H.shape[-1])
            t = jnp.dot(rows, D[:, pl.ds(b * part + at, 2 * LANES)], preferred_element_type=F32)
            t = t.reshape(2, NX, r1 - r0, 2 * LANES)
            own[v % 2, b, :, r0:r1, pl.ds(at, 2 * LANES)] = t[0]
            pair_out[u, b, :, r0:r1, pl.ds(at, 2 * LANES)] = t[1].astype(BF16)
            return carry

        lax.fori_loop(0, part // (2 * LANES), block, 0)
        go(pair_copy(v, b))

    def x_copy(v, b, i):
        u, r0, r1 = STAGES[v]
        d = b % 2 if i != 1 else 1 - b % 2
        at = (u, 3 * b + i, slice(r0, r1))
        return remote(xs.at[at], xr.at[at], x_s.at[v, 3 * b + i], x_r.at[v, 3 * b + i], x_side[d])

    def piece(v, b, k):
        u, r0, r1 = STAGES[v]
        p = lax.rem(x + k + NX, NX)
        return own[v % 2, b, p, r0:r1] + pair_in[u, b, p, r0:r1].astype(F32)

    def x_first(v, b):
        u, r0, r1 = STAGES[v]
        pair_copy(v, b).wait_recv()
        for i, k in ((0, 2), (1, step(b % 2, -1))):
            xs[u, 3 * b + i, r0:r1] = piece(v, b, k).astype(BF16)
            go(x_copy(v, b, i))

    def x_second(v, b):
        u, r0, r1 = STAGES[v]
        x_copy(v, b, 0).wait_recv()
        t = piece(v, b, step(b % 2, 1)) + xr[u, 3 * b, r0:r1].astype(F32)
        xs[u, 3 * b + 2, r0:r1] = t.astype(BF16)
        go(x_copy(v, b, 2))

    def y_copy(v, b):
        u, r0, r1 = STAGES[v]
        return remote(
            ys.at[u, b, r0:r1], yr.at[u, b, r0:r1], y_s.at[v, b], y_r.at[v, b], unit_target[u]
        )

    arrived = set()

    def x_last(v, b):
        u, r0, r1 = STAGES[v]
        t = piece(v, b, 0)
        for i in (1, 2):
            x_copy(v, b, i).wait_recv()
            t = t + xr[u, 3 * b + i, r0:r1].astype(F32)
        if u < UNITS - 1:
            ys[u, b, r0:r1] = t.astype(BF16)
            go(y_copy(v, b))
            return
        if b not in arrived:
            arrived.add(b)
            for other in range(len(STAGES)):
                if STAGES[other][0] < UNITS - 1:
                    y_copy(other, b).wait_recv()
        for other in range(UNITS - 1):
            t = t + yr[other, b, r0:r1].astype(F32)
        out[r0:r1, b * part:(b + 1) * part] = t.astype(BF16)

    steps = {
        CROSS: cross_piece, RELAY: relay_piece, WEIGHT: flatten, SUM: sum_send, END: sum_last, HIDDEN: h_send,
        DOWN: project_down, X1: x_first, X2: x_second, X3: x_last,
    }
    ready, fetched, i = set(), False, AHEAD
    while i < len(ORDER):
        kind, *at = ORDER[i]
        i += 1
        if kind == PRODUCT:
            u, j = at
            if u not in ready:
                ready.add(u)
                rows_ready(u)
            end = j + 1
            while i < len(ORDER) and ORDER[i] == (PRODUCT, u, end):
                end, i = end + 1, i + 1
            project(u, j, end)
            continue
        if kind == DOWN and not fetched:
            fetched = True
            down_copy.wait()
        steps[kind](*at)

    for copy in started:
        copy.wait_send()


def shards(tokens, gate_up_weight, down_weight):
    width = tokens.shape[1]
    units = gate_up_weight.shape[2]
    blocks = units // LANES
    part = width // PARTS
    stages, links = len(STAGES), 7 * len(GROUPS)
    dma = pltpu.SemaphoreType.DMA
    any_space = pl.BlockSpec(memory_space=pl.ANY)
    vmem = pltpu.VMEM
    return pl.pallas_call(
        kernel,
        out_shape=jax.ShapeDtypeStruct((ROWS, width), BF16),
        in_specs=[any_space] * 3,
        out_specs=pl.BlockSpec(memory_space=pltpu.VMEM),
        scratch_shapes=[
            vmem((4, NX, 2, ROWS, width), BF16),
            vmem((blocks, width, 2, LANES), BF16),
            vmem((512, LANES), F32),
            vmem((blocks, width, 2 * LANES), BF16),
            vmem((units, width), BF16),
            vmem((UNITS, NZ, ROWS, 2 * units), F32),
            vmem((UNITS, 7, ROWS, 2 * units), BF16),
            vmem((UNITS, 7, ROWS, 2 * units), BF16),
            vmem((UNITS, NZ, ROWS, units), BF16),
            vmem((2, PARTS, NX, ROWS, part), F32),
            vmem((UNITS, PARTS, NX, ROWS, part), BF16),
            vmem((UNITS, PARTS, NX, ROWS, part), BF16),
            vmem((UNITS, 3 * PARTS, ROWS, part), BF16),
            vmem((UNITS, 3 * PARTS, ROWS, part), BF16),
            vmem((UNITS - 1, PARTS, ROWS, part), BF16),
            vmem((UNITS - 1, PARTS, ROWS, part), BF16),
            dma((3,)),
            dma((blocks,)),
            dma((18,)),
            dma((18,)),
            dma((stages, links)),
            dma((stages, links)),
            dma((stages, links)),
            dma((stages, links)),
            dma((stages, PARTS)),
            dma((stages, PARTS)),
            dma((stages, 3 * PARTS)),
            dma((stages, 3 * PARTS)),
            dma((stages, PARTS)),
            dma((stages, PARTS)),
        ],
        compiler_params=pltpu.CompilerParams(
            collective_id=0, has_side_effects=True, vmem_limit_bytes=62 << 20
        ),
    )(tokens.reshape(NX, 2, ROWS, width), gate_up_weight, down_weight)


def solution(mesh):
    placed = (P("inp", "out"), P("out", None, ("inp", "dep")), P(("inp", "dep"), "out"))
    return jax.shard_map(
        shards, mesh=mesh, in_specs=placed, out_specs=P(("inp", "dep"), "out"), check_vma=False
    )
```
